32 devices in a mesh: gx: 4 (over y, core), gy: 2 (over x), gz: 4 (over z).
Axes of the slice: x: 2, y: 2, z: 4, core: 2. Of those that a mesh axis runs over, the one named last changes fastest.
Arguments:
- populations: float32 [19, 32, 32, 512], P(None, 'gx', 'gy', 'gz'), may hold values from 0 to 1, as said below
- solid_fraction: float32 [32, 32, 512], P('gx', 'gy', 'gz'), may hold values from 0 to 1
- intersection: int32 [32, 32, 512], P('gx', 'gy', 'gz'), may hold values from 0 to 256, as said below
- touch: int32 [4, 2, 4, 256], P('gx', 'gy', 'gz'), may hold values from 0 to 3455, as said below
- particles: float32 [4, 2, 4, 6, 128], P('gx', 'gy', 'gz'), may hold values from -8 to 8, as said below
- contacts: int32 [4, 2, 4, 12, 128], P('gx', 'gy', 'gz'), may hold values from 0 to 3456, as said below
- dest_code: int32 [4, 2, 4, 128], P('gx', 'gy', 'gz'), may hold values from 4 to 22, as said below
- dest_slot: int32 [4, 2, 4, 128], P('gx', 'gy', 'gz'), may hold values from 0 to 127, as said below
Outputs:
- populations_next: float32 [19, 32, 32, 512], P(None, 'gx', 'gy', 'gz')
- particles_next: float32 [4, 2, 4, 6, 128], P('gx', 'gy', 'gz')
The draws below stay inside these ranges and needn't reach their ends.
Inputs may be any that keep to these rules, and one draw needn't show every extreme that they name: intersection = 256 marks a cell that no sphere covers; otherwise a touch slot of the cell's block. `touch`: entry o * 128 + s names slot s of the block at offset o of the 27 neighbouring blocks, offsets ordered with x slowest; the entries of one block are distinct and name every slot of the block itself. `contacts`: 3456 marks an empty entry. `dest_code`: a sphere stays (code 13) or moves one block along one axis (codes 4, 10, 12, 14, 16, 22), never out of the mesh; every slot of every block receives exactly one record. `dest_slot`: see dest_code. `populations`: every population is positive. `particles`: positions, in radii from the block centre, lie within the block's half widths; speeds lie within -1.5 to 1.5.
All inputs are finite; a program needn't handle non-finite values.
Results may differ from the reference program's by a relative error of at most 0.000076.
Values sent between devices are 32-bit elements; how exact they have to be, the bound alone decides.
No kernel may reach another device: no remote copies, remote signals or barrier semaphores. Data moves between devices by JAX's collectives and lax.ppermute only.
A program may use at most 128 MiB of HBM per device.

```python
import jax
import jax.numpy as jnp
from jax import lax

CX = 8
CY = 16
CZ = 128
P_SIZE = 128
NC = 12
R = 8
K = 256
BX = 4
BY = 2
BZ = 4
NX = 32
NY = 32
NZ = 512


LATTICE = [(0, 0, 0), (1, 0, 0), (-1, 0, 0), (0, 1, 0), (0, -1, 0), (0, 0, 1), (0, 0, -1), (1, 1, 0), (-1, -1, 0), (1, -1, 0), (-1, 1, 0), (1, 0, 1), (-1, 0, -1), (1, 0, -1), (-1, 0, 1), (0, 1, 1), (0, -1, -1), (0, 1, -1), (0, -1, 1)]


WEIGHTS = [1.0 / 3.0] + [1.0 / 18.0] * 6 + [1.0 / 36.0] * 12


CONTACT_STEPS = [(1, 0, 0), (-1, 0, 0), (0, 1, 0), (0, -1, 0), (0, 0, 1), (0, 0, -1), (1, 1, 0), (-1, -1, 0), (1, 0, 1), (-1, 0, -1), (0, 1, 1), (0, -1, -1)]


def equilibrium_drawn(density, velocity):
    square = velocity[0] * velocity[0] + velocity[1] * velocity[1] + velocity[2] * velocity[2]
    result = []
    for vector, weight in zip(LATTICE, WEIGHTS):
        projected = vector[0] * velocity[0] + vector[1] * velocity[1] + vector[2] * velocity[2]
        result.append(weight * density * (1.0 + 3.0 * projected + 4.5 * projected * projected - 1.5 * square))
    return jnp.stack(result)


def draw_populations(key, part):
    subkeys = jax.random.split(key, 3)
    grid_shape = (NX, NY, NZ)
    density = 1.0 + 0.02 * jax.random.truncated_normal(subkeys[0], -3.0, 3.0, grid_shape, jnp.float32)
    velocity = 0.04 * jax.random.truncated_normal(subkeys[1], -2.0, 2.0, (3,) + grid_shape, jnp.float32)
    jitter = 1.0 + 0.3 * (jax.random.uniform(subkeys[2], (19,) + grid_shape, jnp.float32) - 0.5)
    return equilibrium_drawn(density, velocity) * jitter


def draw_intersection(key, part):
    subkeys = jax.random.split(jax.random.fold_in(key, 11), 2)
    grid_shape = (NX, NY, NZ)
    height = lax.broadcasted_iota(jnp.int32, grid_shape, 2)
    draw_height = jax.random.randint(subkeys[0], grid_shape, 0, NZ)
    is_solid = draw_height < (NZ - height) * 3 // 4
    chosen = jax.random.randint(subkeys[1], grid_shape, 0, K)
    return jnp.where(is_solid, chosen, K).astype(jnp.int32)


def slot_tables(key):
    folded = jax.random.fold_in(key, 29)
    block_keys = jax.random.split(folded, BX * BY * BZ)
    slot_of_site = jax.vmap(lambda block_key: jax.random.permutation(block_key, P_SIZE))(block_keys)
    slot_of_site = slot_of_site.reshape(BX, BY, BZ, P_SIZE).astype(jnp.int32)
    site_of_slot = jnp.argsort(slot_of_site, axis=-1).astype(jnp.int32)
    return (slot_of_site, site_of_slot)


def neighbour_entry(slot_of_site, site_x, site_y, site_z, home_x, home_y, home_z):
    layers = P_SIZE // 16
    move_x = (site_x + 4) // 4 - 1
    move_y = (site_y + 4) // 4 - 1
    move_z = (site_z + layers) // layers - 1
    block_x = home_x + move_x
    block_y = home_y + move_y
    block_z = home_z + move_z
    inside = (block_x >= 0) & (block_x < BX) & (block_y >= 0) & (block_y < BY) & (block_z >= 0) & (block_z < BZ)
    flat_block = (jnp.clip(block_x, 0, BX - 1) * BY + jnp.clip(block_y, 0, BY - 1)) * BZ + jnp.clip(block_z, 0, BZ - 1)
    local_site = (site_z - layers * move_z) * 16 + (site_y - 4 * move_y) * 4 + site_x - 4 * move_x
    slot_found = slot_of_site.reshape(-1)[flat_block * P_SIZE + local_site]
    code = 9 * (move_x + 1) + 3 * (move_y + 1) + move_z + 1
    return ((code * P_SIZE + slot_found).astype(jnp.int32), inside)


def draw_particles(key, part):
    slot_of_site, site_of_slot = slot_tables(key)
    subkeys = jax.random.split(jax.random.fold_in(key, 13), 2)
    layers = P_SIZE // 16
    spacing_x = CX / (4.0 * R)
    spacing_y = CY / (4.0 * R)
    spacing_z = CZ / (layers * 1.0 * R)
    site_x = (site_of_slot % 4).astype(jnp.float32)
    site_y = (site_of_slot // 4 % 4).astype(jnp.float32)
    site_z = (site_of_slot // 16).astype(jnp.float32)
    centres = jnp.stack([(site_x + 0.5) * spacing_x - CX / (2.0 * R), (site_y + 0.5) * spacing_y - CY / (2.0 * R), (site_z + 0.5) * spacing_z - CZ / (2.0 * R)], axis=3)
    spacing = jnp.array([spacing_x, spacing_y, spacing_z], jnp.float32)
    jitter = jax.random.uniform(subkeys[0], (BX, BY, BZ, 3, P_SIZE), jnp.float32, -0.3, 0.3) * spacing[:, None]
    places = centres + jitter
    speeds = 0.6 * jax.random.truncated_normal(subkeys[1], -2.5, 2.5, (BX, BY, BZ, 3, P_SIZE), jnp.float32)
    return jnp.concatenate([places, speeds], axis=3)


def draw_contacts(key, part):
    slot_of_site, site_of_slot = slot_tables(key)
    shape_here = (BX, BY, BZ, P_SIZE)
    site_x = site_of_slot % 4
    site_y = site_of_slot // 4 % 4
    site_z = site_of_slot // 16
    home_x = lax.broadcasted_iota(jnp.int32, shape_here, 0)
    home_y = lax.broadcasted_iota(jnp.int32, shape_here, 1)
    home_z = lax.broadcasted_iota(jnp.int32, shape_here, 2)
    listed = []
    for step in CONTACT_STEPS:
        entry, inside = neighbour_entry(slot_of_site, site_x + step[0], site_y + step[1], site_z + step[2], home_x, home_y, home_z)
        listed.append(jnp.where(inside, entry, 27 * P_SIZE))
    stacked = jnp.stack(listed, axis=3)
    empty = jax.random.randint(jax.random.fold_in(key, 17), stacked.shape, 0, 4) == 0
    return jnp.where(empty, 27 * P_SIZE, stacked).astype(jnp.int32)


def draw_touch(key, part):
    slot_of_site, unused = slot_tables(key)
    layers = P_SIZE // 16
    extended = 36 * (layers + 2)
    shape_here = (BX, BY, BZ, extended)
    candidate = lax.broadcasted_iota(jnp.int32, shape_here, 3)
    around_x = candidate % 6 - 1
    around_y = candidate // 6 % 6 - 1
    around_z = candidate // 36 - 1
    home_x = lax.broadcasted_iota(jnp.int32, shape_here, 0)
    home_y = lax.broadcasted_iota(jnp.int32, shape_here, 1)
    home_z = lax.broadcasted_iota(jnp.int32, shape_here, 2)
    entry, inside = neighbour_entry(slot_of_site, around_x, around_y, around_z, home_x, home_y, home_z)
    inner = (around_x >= 0) & (around_x < 4) & (around_y >= 0) & (around_y < 4) & (around_z >= 0) & (around_z < layers)
    tier = jnp.where(inner, 0, jnp.where(inside, 1, 2))
    block_count = BX * BY * BZ
    subkeys = jax.random.split(jax.random.fold_in(key, 31), 2)
    ranks = jax.vmap(lambda block_key: jax.random.permutation(block_key, extended))(jax.random.split(subkeys[0], block_count))
    ranks = ranks.reshape(shape_here).astype(jnp.int32)
    order = jnp.argsort(tier * extended + ranks, axis=-1)[..., :K]
    chosen = jnp.take_along_axis(entry, order, axis=-1)
    shuffle = jax.vmap(lambda block_key: jax.random.permutation(block_key, K))(jax.random.split(subkeys[1], block_count))
    shuffle = shuffle.reshape(BX, BY, BZ, K).astype(jnp.int32)
    return jnp.take_along_axis(chosen, shuffle, axis=-1).astype(jnp.int32)


def migration_plan(key):
    folded = jax.random.fold_in(key, 23)
    subkeys = jax.random.split(folded, 7)
    counts = [BX, BY, BZ]
    shape_here = (BX, BY, BZ, P_SIZE)
    slot_ids = lax.broadcasted_iota(jnp.int32, shape_here, 3)
    moves = []
    for dimension in range(3):
        parity = jax.random.randint(subkeys[dimension], (), 0, 2)
        amount = jax.random.randint(subkeys[3 + dimension], (), max(P_SIZE // 16, 1), P_SIZE // 4 + 1)
        coordinate = lax.broadcasted_iota(jnp.int32, shape_here, dimension)
        first_slot = dimension * (P_SIZE // 4)
        chosen = (slot_ids >= first_slot) & (slot_ids < first_slot + amount)
        upward = ((coordinate - parity) % 2 == 0) & (coordinate + 1 < counts[dimension])
        downward = ((coordinate - parity) % 2 == 1) & (coordinate >= 1)
        moves.append(jnp.where(chosen, upward.astype(jnp.int32) - downward.astype(jnp.int32), 0))
    codes = 13 + 9 * moves[0] + 3 * moves[1] + moves[2]
    block_count = BX * BY * BZ
    perms = jax.vmap(lambda block_key: jax.random.permutation(block_key, P_SIZE))(jax.random.split(subkeys[6], block_count))
    home_x = lax.broadcasted_iota(jnp.int32, shape_here, 0)
    home_y = lax.broadcasted_iota(jnp.int32, shape_here, 1)
    home_z = lax.broadcasted_iota(jnp.int32, shape_here, 2)
    target = ((home_x + moves[0]) * BY + home_y + moves[1]) * BZ + home_z + moves[2]
    slots_new = perms.reshape(-1)[target * P_SIZE + slot_ids]
    return (codes.astype(jnp.int32), slots_new.astype(jnp.int32))


def draw_dest_code(key, part):
    return migration_plan(key)[0]


def draw_dest_slot(key, part):
    return migration_plan(key)[1]


def block_levels(own_key, shape, pieces, smallest, high):
    loudness, own = 1.0, jax.random.fold_in(own_key, 6)
    for position, blocks in pieces:
        steps = jnp.exp(jax.random.uniform(jax.random.fold_in(own, position), (blocks,), jnp.float32, smallest / len(pieces), high / len(pieces)))
        loudness = loudness * jnp.repeat(steps, shape[position] // blocks).reshape([-1 if axis == position else 1 for axis in range(len(shape))])
    return loudness


def setup_inputs(seed: int = 0) -> dict:
    arg_keys = jax.random.split(jax.random.key(seed), 9)
    return {
        "populations": draw_populations(jax.random.fold_in(arg_keys[8], 71), 0),
        "solid_fraction": jnp.clip(1.0 * jax.random.uniform(arg_keys[1], (NX, NY, NZ), jnp.float32) ** block_levels(arg_keys[1], (NX, NY, NZ), ((0, 4), (1, 2), (2, 4)), -0.2, 0.2), 0.0, 1.0),
        "intersection": draw_intersection(jax.random.fold_in(arg_keys[8], 71), 0),
        "touch": draw_touch(jax.random.fold_in(arg_keys[8], 71), 0),
        "particles": draw_particles(jax.random.fold_in(arg_keys[8], 71), 0),
        "contacts": draw_contacts(jax.random.fold_in(arg_keys[8], 71), 0),
        "dest_code": draw_dest_code(jax.random.fold_in(arg_keys[8], 71), 0),
        "dest_slot": draw_dest_slot(jax.random.fold_in(arg_keys[8], 71), 0),
    }


LATTICE = [(0, 0, 0), (1, 0, 0), (-1, 0, 0), (0, 1, 0), (0, -1, 0), (0, 0, 1), (0, 0, -1),
           (1, 1, 0), (-1, -1, 0), (1, -1, 0), (-1, 1, 0), (1, 0, 1), (-1, 0, -1),
           (1, 0, -1), (-1, 0, 1), (0, 1, 1), (0, -1, -1), (0, 1, -1), (0, -1, 1)]
OPPOSITE = [0, 2, 1, 4, 3, 6, 5, 8, 7, 10, 9, 12, 11, 14, 13, 16, 15, 18, 17]
WEIGHTS = [1.0 / 3.0] + [1.0 / 18.0] * 6 + [1.0 / 36.0] * 12
RELAX_TIME = 0.8
SPEED_UNIT = 0.05
FORCE_SCALE = 0.1
CONTACT_GAIN = 1.0
GRAVITY_STEP = 0.1


def equilibrium(density, velocity):
    square = velocity[0] * velocity[0] + velocity[1] * velocity[1] + velocity[2] * velocity[2]
    result = []
    for vector, weight in zip(LATTICE, WEIGHTS):
        projected = vector[0] * velocity[0] + vector[1] * velocity[1] + vector[2] * velocity[2]
        result.append(weight * density * (1.0 + 3.0 * projected + 4.5 * projected * projected - 1.5 * square))
    return jnp.stack(result)


def collide(populations, solid_weight, solid_velocity):
    lattice_table = jnp.array(LATTICE, jnp.float32)
    density = jnp.sum(populations, axis=0)
    momentum = jnp.tensordot(lattice_table.T, populations, axes=1, precision=lax.Precision.HIGHEST)
    velocity = momentum / density
    fluid_eq = equilibrium(density, velocity)
    solid_eq = equilibrium(density, solid_velocity)
    mirrored = jnp.stack([populations[mirror_index] for mirror_index in OPPOSITE])
    fluid_mirror = jnp.stack([fluid_eq[mirror_index] for mirror_index in OPPOSITE])
    exchange_term = mirrored - populations + solid_eq - fluid_mirror
    relaxed = populations - (1.0 - solid_weight) / RELAX_TIME * (populations - fluid_eq) + solid_weight * exchange_term
    cell_force = -jnp.tensordot(lattice_table.T, solid_weight * exchange_term, axes=1, precision=lax.Precision.HIGHEST)
    return relaxed, cell_force


def block_offsets(entries, slots_each, span_x, span_y, span_z, radius):
    block_code = jnp.arange(entries, dtype=jnp.int32) // slots_each
    return jnp.stack([(block_code // 9 - 1).astype(jnp.float32) * (span_x / radius),
                      ((block_code // 3) % 3 - 1).astype(jnp.float32) * (span_y / radius),
                      (block_code % 3 - 1).astype(jnp.float32) * (span_z / radius)])


def reference(populations, solid_fraction, intersection, touch, particles, contacts, dest_code, dest_slot):
    blocks = BX * BY * BZ
    padded = jnp.pad(particles, ((1, 1), (1, 1), (1, 1), (0, 0), (0, 0)))
    neighbourhood = jnp.stack([padded[step_x:step_x + BX, step_y:step_y + BY, step_z:step_z + BZ]
                               for step_x in range(3) for step_y in range(3) for step_z in range(3)], axis=3)
    records_near = jnp.moveaxis(neighbourhood, 4, 3).reshape(blocks, 6, 27 * P_SIZE)
    touch_rows = touch.reshape(blocks, K)
    touch_velocity = jnp.take_along_axis(records_near[:, 3:6, :], jnp.broadcast_to(touch_rows[:, None, :], (blocks, 3, K)), axis=2)
    touch_velocity = jnp.concatenate([touch_velocity, jnp.zeros((blocks, 3, 1), jnp.float32)], axis=2)
    velocity_rows = jnp.transpose(touch_velocity, (0, 2, 1)).reshape(blocks * (K + 1), 3)
    block_x = (jnp.arange(NX, dtype=jnp.int32) // CX)[:, None, None]
    block_y = (jnp.arange(NY, dtype=jnp.int32) // CY)[None, :, None]
    block_z = (jnp.arange(NZ, dtype=jnp.int32) // CZ)[None, None, :]
    slot_rows = ((block_x * BY + block_y) * BZ + block_z) * (K + 1) + intersection
    fraction_term = jnp.where(intersection < K, solid_fraction * (RELAX_TIME - 0.5) / ((1.0 - solid_fraction) + (RELAX_TIME - 0.5)), jnp.float32(0.0))

    def slab_step(start):
        slab_pop = lax.dynamic_slice_in_dim(populations, start, CX, 1)
        slab_rows = lax.dynamic_slice_in_dim(slot_rows, start, CX, 0)
        slab_weight = lax.dynamic_slice_in_dim(fraction_term, start, CX, 0)
        solid_velocity = SPEED_UNIT * jnp.moveaxis(velocity_rows[slab_rows], -1, 0)
        return collide(slab_pop, slab_weight, solid_velocity)

    relaxed, cell_force = lax.map(slab_step, jnp.arange(BX, dtype=jnp.int32) * CX)
    relaxed = jnp.moveaxis(relaxed, 0, 1).reshape(19, NX, NY, NZ)
    cell_force = jnp.moveaxis(cell_force, 0, 1).reshape(3, NX, NY, NZ)

    coord_x = jnp.arange(NX, dtype=jnp.int32)[:, None, None]
    coord_y = jnp.arange(NY, dtype=jnp.int32)[None, :, None]
    coord_z = jnp.arange(NZ, dtype=jnp.int32)[None, None, :]
    passed = []
    for direction, vector in enumerate(LATTICE):
        rolled = jnp.roll(relaxed[direction], vector, axis=(0, 1, 2))
        inside = ((coord_x - vector[0] >= 0) & (coord_x - vector[0] < NX) & (coord_y - vector[1] >= 0)
                  & (coord_y - vector[1] < NY) & (coord_z - vector[2] >= 0) & (coord_z - vector[2] < NZ))
        passed.append(jnp.where(inside, rolled, relaxed[OPPOSITE[direction]]))
    populations_next = jnp.stack(passed)

    touch_force = jax.ops.segment_sum(cell_force.reshape(3, -1).T, slot_rows.reshape(-1), num_segments=blocks * (K + 1))
    touch_force = touch_force.reshape(blocks, K + 1, 3)[:, :K, :]
    owner_x = lax.broadcasted_iota(jnp.int32, (BX, BY, BZ, K), 0).reshape(blocks, K)
    owner_y = lax.broadcasted_iota(jnp.int32, (BX, BY, BZ, K), 1).reshape(blocks, K)
    owner_z = lax.broadcasted_iota(jnp.int32, (BX, BY, BZ, K), 2).reshape(blocks, K)
    touch_code = touch_rows // P_SIZE
    owner_rows = (((owner_x + touch_code // 9) * (BY + 2) + owner_y + (touch_code // 3) % 3) * (BZ + 2)
                  + owner_z + touch_code % 3) * P_SIZE + touch_rows % P_SIZE
    hydro = jax.ops.segment_sum(touch_force.reshape(-1, 3), owner_rows.reshape(-1), num_segments=(BX + 2) * (BY + 2) * (BZ + 2) * P_SIZE)
    hydro = hydro.reshape(BX + 2, BY + 2, BZ + 2, P_SIZE, 3)[1:-1, 1:-1, 1:-1]
    hydro = jnp.moveaxis(hydro, -1, 3).reshape(blocks, 3, P_SIZE)

    offsets = block_offsets(27 * P_SIZE + 1, P_SIZE, CX, CY, CZ, R)
    partner_table = jnp.concatenate([records_near[:, 0:3, :], jnp.zeros((blocks, 3, 1), jnp.float32)], axis=2) + offsets[None]
    contact_rows = contacts.reshape(blocks, NC, P_SIZE)
    partner = jax.vmap(lambda table_block, rows_block: jnp.take(table_block, rows_block, axis=1))(partner_table, contact_rows)
    own_records = particles.reshape(blocks, 6, P_SIZE)
    separation = own_records[:, 0:3, None, :] - partner
    valid = (contact_rows < 27 * P_SIZE).astype(jnp.float32)
    square = jnp.sum(separation * separation, axis=1)
    soften = 1.0 + 0.25 * square
    strength = CONTACT_GAIN * valid / (soften * soften)
    contact_force = jnp.sum(separation * strength[:, None], axis=2)
    gravity = jnp.array([0.0, 0.0, GRAVITY_STEP], jnp.float32)
    velocity_new = own_records[:, 3:6] + FORCE_SCALE * hydro + contact_force - gravity[None, :, None]
    position_new = own_records[:, 0:3] + velocity_new * (SPEED_UNIT / R)

    dest_codes = dest_code.reshape(blocks, P_SIZE)
    move_x = dest_codes // 9 - 1
    move_y = (dest_codes // 3) % 3 - 1
    move_z = dest_codes % 3 - 1
    shifted = position_new - jnp.stack([move_x.astype(jnp.float32) * (CX / R), move_y.astype(jnp.float32) * (CY / R),
                                        move_z.astype(jnp.float32) * (CZ / R)], axis=1)
    record = jnp.concatenate([shifted, velocity_new], axis=1)
    home_x = owner_x[:, 0:1]
    home_y = owner_y[:, 0:1]
    home_z = owner_z[:, 0:1]
    target = (((home_x + move_x) * BY + home_y + move_y) * BZ + home_z + move_z) * P_SIZE + dest_slot.reshape(blocks, P_SIZE)
    arrived = jax.ops.segment_sum(jnp.transpose(record, (0, 2, 1)).reshape(-1, 6), target.reshape(-1), num_segments=blocks * P_SIZE)
    arrived = jnp.moveaxis(arrived.reshape(BX, BY, BZ, P_SIZE, 6), -1, 3)
    return populations_next, arrived
```

```python
import jax
import jax.numpy as jnp
from jax import lax
from jax.experimental import pallas as pl
from jax.experimental.pallas import tpu as pltpu
from jax.sharding import PartitionSpec as P

R = 8


LATTICE = [
    (0, 0, 0),
    (1, 0, 0),
    (-1, 0, 0),
    (0, 1, 0),
    (0, -1, 0),
    (0, 0, 1),
    (0, 0, -1),
    (1, 1, 0),
    (-1, -1, 0),
    (1, -1, 0),
    (-1, 1, 0),
    (1, 0, 1),
    (-1, 0, -1),
    (1, 0, -1),
    (-1, 0, 1),
    (0, 1, 1),
    (0, -1, -1),
    (0, 1, -1),
    (0, -1, 1),
]
OPPOSITE = [0, 2, 1, 4, 3, 6, 5, 8, 7, 10, 9, 12, 11, 14, 13, 16, 15, 18, 17]
WEIGHTS = [1.0 / 3.0] + [1.0 / 18.0] * 6 + [1.0 / 36.0] * 12
RELAX_TIME = 0.8
SPEED_UNIT = 0.05
FORCE_SCALE = 0.1
CONTACT_GAIN = 1.0
GRAVITY_STEP = 0.1


F32 = jnp.float32
BF16 = jnp.bfloat16
SIDES = [[[i for i, c in enumerate(LATTICE) if c[dim] == sign] for sign in (-1, 1)] for dim in range(3)]
Z_DIRS = SIDES[2][1] + SIDES[2][0]
FACES = [(1, 0, 0), (-1, 0, 0), (0, 1, 0), (0, -1, 0), (0, 0, 1), (0, 0, -1)]
NT = (((1,), (1,)), ((), ()))


def outgoing(dim, sign):
    return SIDES[dim][1 if sign > 0 else 0]


def find(vector):
    return LATTICE.index(tuple(vector))


def split3(value):
    high = value.astype(BF16).astype(F32)
    rest = value - high
    middle = rest.astype(BF16).astype(F32)
    return high, middle, rest - middle


def solid_share(fraction, slots, touches):
    return jnp.where(
        slots < touches,
        fraction * (RELAX_TIME - 0.5) / (1.0 - fraction + (RELAX_TIME - 0.5)),
        0.0,
    )


def moments(f):
    density = f[0]
    for i in range(1, 19):
        density = density + f[i]
    momentum = []
    for dim in range(3):
        total = None
        for i in outgoing(dim, 1):
            pair = f[i] - f[OPPOSITE[i]]
            total = pair if total is None else total + pair
        momentum.append(total)
    return density, momentum


def sums_kernel(pop, fraction, slots, particles, touch, packet, vals, *, span_x, span_y, touches):
    width = pop.shape[2]
    for x in range(span_x):
        rows = pl.ds(x * span_y, span_y)
        f = [pop[i, rows, :] for i in range(19)]
        density, momentum = moments(f)
        share = solid_share(fraction[rows, :], slots[rows, :], touches)
        for q, field in enumerate(momentum + [density]):
            for s, part in enumerate(split3(share * field)):
                vals[pl.ds(x * span_y * 16 + s * 4 + q, span_y, stride=16), :] = part
        for j in range(12, 16):
            vals[pl.ds(x * span_y * 16 + j, span_y, stride=16), :] = jnp.zeros((span_y, width), F32)
    labels = lax.broadcasted_iota(jnp.int32, (touches, width), 0)
    group = 8

    def step(turn, total):
        block = slots[pl.ds(turn * group, group), :]
        left = []
        right = []
        for r in range(group):
            left.append(vals[pl.ds((turn * group + r) * 16, 16), :].astype(BF16))
            right.append(jnp.where(block[r : r + 1, :] == labels, 1.0, 0.0).astype(BF16))
        return total + lax.dot_general(
            jnp.concatenate(left, axis=1),
            jnp.concatenate(right, axis=1),
            NT,
            preferred_element_type=F32,
        )

    turns = span_x * span_y // group
    total = lax.fori_loop(0, turns, step, jnp.zeros((16, touches), F32), unroll=2)
    sums = total[0:4] + total[4:8] + total[8:12]
    halves = touches // width
    packet[0:6, :] = particles[...]
    packet[6 : 6 + halves, :] = touch[...].astype(F32)
    for h in range(halves):
        packet[6 + halves + 4 * h : 10 + halves + 4 * h, :] = sums[:, h * width : (h + 1) * width]


def lookup(table, index):
    return jnp.take_along_axis(table, index, axis=1)


def step_kernel(
    place, pop, fraction, slots, packets, touch, contacts, code, slot,
    relaxed, send, z_up, z_down, stay, speeds, columns,
    *, span_x, span_y, touches, mesh_shape,
):
    width = pop.shape[2]
    halves = touches // width
    neighbours = contacts.shape[0]
    n_x, n_y, n_z = mesh_shape
    lane = lax.broadcasted_iota(jnp.int32, (8, width), 1)
    sub = lax.broadcasted_iota(jnp.int32, (8, width), 0)
    base = packets.shape[1]
    me = (place[0] * n_y + place[1]) * n_z + place[2]
    own = packets[me, 0:8, :]
    tables = []
    labels = lax.broadcasted_iota(jnp.int32, (width, width), 0)
    force = [jnp.zeros((24, width), F32) for h in range(halves)]
    touched = [jnp.zeros((8, width), F32) for h in range(halves)]
    touch_entries = [touch[h : h + 1, :] for h in range(halves)]
    touch_code = [jnp.broadcast_to(t // width, (8, width)) for t in touch_entries]
    touch_slot = [jnp.broadcast_to(t % width, (8, width)) for t in touch_entries]
    contact_all = contacts[...]
    contact_code = contact_all // width
    contact_slot = contact_all % width
    picked = [jnp.zeros((8, width), F32) for n in range(neighbours)]
    shifts = (span_x / R, span_y / R, width / R)
    for c in range(27):
        o = (c // 9 - 1, c // 3 % 3 - 1, c % 3 - 1)
        p = [place[k] + o[k] for k in range(3)]
        valid = (
            (p[0] >= 0) & (p[0] < n_x) & (p[1] >= 0) & (p[1] < n_y) & (p[2] >= 0) & (p[2] < n_z)
        )
        index = jnp.where(valid, (p[0] * n_y + p[1]) * n_z + p[2], me)
        keep = valid.astype(F32)
        record = packets[index, 0:8, :] * keep
        for h in range(halves):
            got = lookup(record, touch_slot[h])
            touched[h] = jnp.where(touch_code[h] == c, got, touched[h])
        offset = jnp.where(sub == 0, o[0] * shifts[0], jnp.where(sub == 1, o[1] * shifts[1], jnp.where(sub == 2, o[2] * shifts[2], 0.0)))
        shifted = record + offset
        for n in range(neighbours):
            got = lookup(shifted, jnp.broadcast_to(contact_slot[n : n + 1, :], (8, width)))
            picked[n] = jnp.where(jnp.broadcast_to(contact_code[n : n + 1, :], (8, width)) == c, got, picked[n])
        entries = packets[index, 6 : 6 + halves, :].astype(jnp.int32)
        mine = jnp.where(entries // width == 26 - c, entries % width, -1)
        for h in range(halves):
            part = packets[index, 6 + halves + 4 * h : 10 + halves + 4 * h, :] * keep
            part = jnp.concatenate([part, jnp.zeros((4, width), F32)], axis=0)
            left = jnp.concatenate(list(split3(part)), axis=0).astype(BF16)
            right = jnp.where(mine[h : h + 1, :] == labels, 1.0, 0.0).astype(BF16)
            force[h] = force[h] + lax.dot_general(left, right, NT, preferred_element_type=F32)
    total = force[0]
    for h in range(1, halves):
        total = total + force[h]
    total = total[0:8] + total[8:16] + total[16:24]

    contact_force = jnp.zeros((8, width), F32)
    for n in range(neighbours):
        separation = jnp.where(sub < 3, own - picked[n], 0.0)
        square = jnp.sum(separation * separation, axis=0, keepdims=True)
        soften = 1.0 + 0.25 * square
        valid = jnp.where(contact_all[n : n + 1, :] < 27 * width, CONTACT_GAIN, 0.0)
        contact_force = contact_force + separation * (valid / (soften * soften))
    position = own[0:3]
    velocity = own[3:6]
    hydro = total[0:3] - SPEED_UNIT * velocity * total[3:4]
    gravity = jnp.where(sub[0:3] == 2, GRAVITY_STEP, 0.0)
    velocity_new = velocity + FORCE_SCALE * hydro + contact_force[0:3] - gravity
    position_new = position + velocity_new * (SPEED_UNIT / R)
    record = jnp.concatenate([position_new, velocity_new, jnp.zeros((2, width), F32)], axis=0)
    placing = jnp.where(slot[...] == labels, 1.0, 0.0).astype(BF16)
    arrive = []
    for o in [(0, 0, 0)] + FACES:
        offset = jnp.where(sub == 0, o[0] * shifts[0], jnp.where(sub == 1, o[1] * shifts[1], jnp.where(sub == 2, o[2] * shifts[2], 0.0)))
        chosen = jnp.where(code[...] == 13 + 9 * o[0] + 3 * o[1] + o[2], record - offset, 0.0)
        left = jnp.concatenate(list(split3(chosen)), axis=0).astype(BF16)
        out = lax.dot_general(left, placing, NT, preferred_element_type=F32)
        arrive.append(out[0:8] + out[8:16] + out[16:24])
    stay[...] = arrive[0]

    for h in range(halves):
        speeds[h, :, :] = SPEED_UNIT * touched[h]
    lane_y = lax.broadcasted_iota(jnp.int32, (span_y, width), 1)

    def slab(x, carry):
        rows = pl.ds(pl.multiple_of(x * span_y, span_y), span_y)
        f = [pop[i, rows, :] for i in range(19)]
        density, momentum = moments(f)
        index = slots[rows, :]
        share = solid_share(fraction[rows, :], index, touches)
        solid = []
        for dim in range(3):
            value = jnp.zeros((span_y, width), F32)
            for h in range(halves):
                line = jnp.broadcast_to(speeds[h, 3 + dim : 4 + dim, :], (span_y, width))
                got = lookup(line, index % width)
                value = jnp.where(index // width == h, got, value)
            solid.append(value)
        u = [m / density for m in momentum]
        rate = (1.0 - share) / RELAX_TIME
        fluid_base = 1.0 - 1.5 * (u[0] * u[0] + u[1] * u[1] + u[2] * u[2])
        solid_base = 1.0 - 1.5 * (solid[0] * solid[0] + solid[1] * solid[1] + solid[2] * solid[2])

        def project(i, v):
            value = None
            for dim in range(3):
                if LATTICE[i][dim]:
                    term = v[dim] if LATTICE[i][dim] > 0 else -v[dim]
                    value = term if value is None else value + term
            return value

        packed = jnp.zeros((span_y, width), F32)
        for i in range(19):
            j = OPPOSITE[i]
            if j < i:
                continue
            scale = WEIGHTS[i] * density
            if i == 0:
                fluid = scale * fluid_base
                results = [(0, f[0] - rate * (f[0] - fluid) + share * (scale * solid_base - fluid))]
            else:
                pu = project(i, u)
                ps = project(i, solid)
                even_u = fluid_base + 4.5 * pu * pu
                even_s = solid_base + 4.5 * ps * ps
                eq_i = scale * (even_u + 3.0 * pu)
                eq_j = scale * (even_u - 3.0 * pu)
                solid_i = scale * (even_s + 3.0 * ps)
                solid_j = scale * (even_s - 3.0 * ps)
                swap = f[j] - f[i]
                results = [
                    (i, f[i] - rate * (f[i] - eq_i) + share * (swap + solid_i - eq_j)),
                    (j, f[j] - rate * (f[j] - eq_j) + share * (solid_j - swap - eq_i)),
                ]
            for d, value in results:
                relaxed[d, rows, :] = value
                if LATTICE[d][2]:
                    k = Z_DIRS.index(d)
                    at = width - 1 if LATTICE[d][2] > 0 else 0
                    packed = jnp.where(lane_y == k, pltpu.roll(value, (k - at) % width, 1), packed)
        columns[rows, :] = packed
        return carry

    lax.fori_loop(0, span_x, slab, 0)
    z_rows = columns[...].T[0:16, :]
    z_up[0:8, :] = arrive[5]
    z_up[8:16, :] = jnp.concatenate([z_rows[0:5], jnp.zeros((3, width), F32)], axis=0)
    z_down[0:8, :] = arrive[6]
    z_down[8:16, :] = jnp.concatenate([z_rows[5:10], jnp.zeros((3, width), F32)], axis=0)
    send[...] = jnp.zeros(send.shape, F32)
    for o_x in (-1, 0, 1):
        for o_y in (-1, 0, 1):
            if o_x == 0 and o_y == 0:
                continue
            p_x = place[0] + o_x
            p_y = place[1] + o_y
            valid = (p_x >= 0) & (p_x < n_x) & (p_y >= 0) & (p_y < n_y)

            @pl.when(valid)
            def fill(o_x=o_x, o_y=o_y, index=p_x * n_y + p_y):
                x_at = span_x - 1 if o_x > 0 else 0
                y_at = span_y - 1 if o_y > 0 else 0
                if o_x and o_y:
                    row = x_at * span_y + y_at
                    send[index, 8:9, :] = relaxed[find((o_x, o_y, 0)), row : row + 1, :]
                    return
                n = FACES.index((o_x, o_y, 0))
                up = Z_DIRS.index(find((o_x, o_y, 1)))
                down = Z_DIRS.index(find((o_x, o_y, -1)))
                send[index, 0:8, :] = jnp.concatenate(
                    [arrive[1 + n][0:6], z_rows[up : up + 1], z_rows[down : down + 1]], axis=0
                )
                if o_x:
                    for k, d in enumerate(outgoing(0, o_x)):
                        send[index, 8 + k * span_y : 8 + (k + 1) * span_y, :] = relaxed[
                            d, x_at * span_y : (x_at + 1) * span_y, :
                        ]
                else:
                    for k, d in enumerate(outgoing(1, o_y)):
                        send[index, 8 + k * span_x : 8 + (k + 1) * span_x, :] = relaxed[
                            d, pl.ds(y_at, span_x, stride=span_y), :
                        ]


def pass_kernel(
    place, relaxed, got, z_below, z_above, stay, out, particles, filler,
    *, span_x, span_y, mesh_shape,
):
    width = relaxed.shape[2]
    n_x, n_y, n_z = mesh_shape
    cells = span_x * span_y

    def neighbour(o_x, o_y):
        p_x = jnp.clip(place[0] + o_x, 0, n_x - 1)
        p_y = jnp.clip(place[1] + o_y, 0, n_y - 1)
        return p_x * n_y + p_y

    def inside(axis, sign):
        p = place[axis] + sign
        return (p >= 0) & (p < mesh_shape[axis])

    arrived = stay[...] + z_below[0:8, :] + z_above[0:8, :]
    for o_x, o_y, o_z in FACES[:4]:
        axis = 0 if o_x else 1
        keep = inside(axis, o_x + o_y)
        arrived = arrived + jnp.where(keep, got[neighbour(o_x, o_y), 0:8, :], 0.0)
    particles[...] = arrived[0:6]

    lane1 = lax.broadcasted_iota(jnp.int32, (1, cells), 1)
    fills = []
    for d in Z_DIRS:
        c_x, c_y, c_z = LATTICE[d]
        source = z_below if c_z > 0 else z_above
        k = outgoing(2, c_z).index(d)
        row = source[8 + k : 9 + k, :]
        if c_x or c_y:
            edge = source[pl.ds(16 + neighbour(-c_x, -c_y), 1), :]
            if c_x:
                row = pltpu.roll(row, (c_x * span_y) % cells, 1)
                edge = pltpu.roll(edge, (c_x * span_y) % cells, 1)
                at_edge = lane1 < span_y if c_x > 0 else lane1 >= cells - span_y
            else:
                row = pltpu.roll(row, c_y % cells, 1)
                edge = pltpu.roll(edge, (-c_y * (span_y - 1)) % cells, 1)
                at_edge = lane1 % span_y == (0 if c_y > 0 else span_y - 1)
            row = jnp.where(at_edge, edge, row)
        fills.append(row)
    stacked = jnp.concatenate(fills + [jnp.zeros((cells - len(fills), cells), F32)], axis=0)
    filler[...] = stacked.T
    lane = lax.broadcasted_iota(jnp.int32, (span_y, width), 1)
    line = lax.broadcasted_iota(jnp.int32, (span_y, width), 0)
    for d, (c_x, c_y, c_z) in enumerate(LATTICE):
        y_in = inside(1, -c_y) if c_y else None
        z_in = inside(2, -c_z) if c_z else None
        for x in range(span_x):
            x_from = x - c_x
            crosses = x_from < 0 or x_from >= span_x
            if crosses:
                k = outgoing(0, c_x).index(d)
                value = got[neighbour(-c_x, 0), 8 + k * span_y : 8 + (k + 1) * span_y, :]
            else:
                value = relaxed[d, x_from * span_y : (x_from + 1) * span_y, :]
            outside = None
            if c_y:
                if crosses:
                    row = got[neighbour(-c_x, -c_y), 8:9, :]
                else:
                    at = 8 + outgoing(1, c_y).index(d) * span_x + x_from
                    row = got[neighbour(0, -c_y), at : at + 1, :]
                at_edge = line == (0 if c_y > 0 else span_y - 1)
                value = jnp.where(at_edge, row, pltpu.roll(value, c_y % span_y, 0))
                outside = at_edge & jnp.logical_not(y_in)
            if c_z:
                target = 0 if c_z > 0 else width - 1
                fill = pltpu.roll(
                    filler[x * span_y : (x + 1) * span_y, :], (target - Z_DIRS.index(d)) % width, 1
                )
                at_edge = lane == target
                value = jnp.where(at_edge, fill, pltpu.roll(value, c_z % width, 1))
                z_out = at_edge & jnp.logical_not(z_in)
                outside = z_out if outside is None else outside | z_out
            if crosses:
                x_out = jnp.broadcast_to(jnp.logical_not(inside(0, -c_x)), (span_y, width))
                outside = x_out if outside is None else outside | x_out
            if outside is not None:
                back = relaxed[OPPOSITE[d], x * span_y : (x + 1) * span_y, :]
                value = jnp.where(outside, back, value)
            out[d, x * span_y : (x + 1) * span_y, :] = value


def shape_of(*dims):
    return jax.ShapeDtypeStruct(dims, F32)


def call(kernel, outs, scratch, smem, *operands):
    vmem = pl.BlockSpec(memory_space=pltpu.VMEM)
    specs = [pl.BlockSpec(memory_space=pltpu.SMEM)] * smem + [vmem] * (len(operands) - smem)
    return pl.pallas_call(
        kernel,
        out_shape=outs,
        in_specs=specs,
        out_specs=jax.tree.map(lambda unused: vmem, outs),
        scratch_shapes=scratch,
    )(*operands)


def bind(kernel, **settings):
    def bound(*refs):
        return kernel(*refs, **settings)

    return bound


def body(
    populations, solid_fraction, intersection, touch, particles, contacts, dest_code, dest_slot
):
    unused, span_x, span_y, span_z = populations.shape
    particle_slots = particles.shape[4]
    touches = touch.shape[3]
    halves = touches // span_z
    neighbours = contacts.shape[3]
    cells = span_x * span_y
    axes = ("gx", "gy", "gz")
    mesh_shape = tuple(lax.axis_size(axis) for axis in axes)
    n_x, n_y, n_z = mesh_shape
    place = jnp.stack([lax.axis_index(axis) for axis in axes]).astype(jnp.int32)
    pop = populations.reshape(19, cells, span_z)
    fraction = solid_fraction.reshape(cells, span_z)
    slots = intersection.reshape(cells, span_z)
    records = particles.reshape(6, particle_slots)
    touch_rows = touch.reshape(halves, span_z)
    rows = 6 + 5 * halves
    packet = call(
        bind(sums_kernel, span_x=span_x, span_y=span_y, touches=touches),
        shape_of(rows, span_z),
        [pltpu.VMEM((cells * 16, span_z), F32)],
        0,
        pop, fraction, slots, records, touch_rows,
    )
    copies = jnp.broadcast_to(packet[None], (n_x * n_y * n_z, rows, span_z))
    packets = lax.all_to_all(copies, axes, 0, 0)
    chunk = 8 + 5 * max(span_x, span_y)
    relaxed, send, z_up, z_down, stay = call(
        bind(step_kernel, span_x=span_x, span_y=span_y, touches=touches, mesh_shape=mesh_shape),
        (
            shape_of(19, cells, span_z),
            shape_of(n_x * n_y, chunk, span_z),
            shape_of(16, span_z),
            shape_of(16, span_z),
            shape_of(8, span_z),
        ),
        [pltpu.VMEM((halves, 8, span_z), F32), pltpu.VMEM((cells, span_z), F32)],
        1,
        place, pop, fraction, slots, packets, touch_rows,
        contacts.reshape(neighbours, particle_slots),
        dest_code.reshape(1, particle_slots), dest_slot.reshape(1, particle_slots),
    )
    got = lax.all_to_all(send, ("gx", "gy"), 0, 0)
    up = [(i, i + 1) for i in range(n_z - 1)]
    down = [(j, i) for i, j in up]
    z_below = lax.ppermute(jnp.concatenate([z_up, got[:, 6]]), "gz", up)
    z_above = lax.ppermute(jnp.concatenate([z_down, got[:, 7]]), "gz", down)
    passed, arrived = call(
        bind(pass_kernel, span_x=span_x, span_y=span_y, mesh_shape=mesh_shape),
        (shape_of(19, cells, span_z), shape_of(6, span_z)),
        [pltpu.VMEM((cells, cells), F32)],
        1,
        place, relaxed, got, z_below, z_above, stay,
    )
    return passed.reshape(populations.shape), arrived.reshape(1, 1, 1, 6, particle_slots)


def solution(mesh):
    placed = (
        P(None, "gx", "gy", "gz"),
        P("gx", "gy", "gz"),
        P("gx", "gy", "gz"),
        P("gx", "gy", "gz", None),
        P("gx", "gy", "gz", None, None),
        P("gx", "gy", "gz", None, None),
        P("gx", "gy", "gz", None),
        P("gx", "gy", "gz", None),
    )
    return jax.shard_map(
        body,
        mesh=mesh,
        in_specs=placed,
        out_specs=(P(None, "gx", "gy", "gz"), P("gx", "gy", "gz", None, None)),
        check_vma=False,
    )
```

```python
import jax
import jax.numpy as jnp
from jax import lax
from jax.experimental import pallas as pl
from jax.experimental.pallas import tpu as pltpu
from jax.sharding import PartitionSpec as P

R = 8


LATTICE = [
    (0, 0, 0),
    (1, 0, 0),
    (-1, 0, 0),
    (0, 1, 0),
    (0, -1, 0),
    (0, 0, 1),
    (0, 0, -1),
    (1, 1, 0),
    (-1, -1, 0),
    (1, -1, 0),
    (-1, 1, 0),
    (1, 0, 1),
    (-1, 0, -1),
    (1, 0, -1),
    (-1, 0, 1),
    (0, 1, 1),
    (0, -1, -1),
    (0, 1, -1),
    (0, -1, 1),
]
OPPOSITE = [0, 2, 1, 4, 3, 6, 5, 8, 7, 10, 9, 12, 11, 14, 13, 16, 15, 18, 17]
WEIGHTS = [1.0 / 3.0] + [1.0 / 18.0] * 6 + [1.0 / 36.0] * 12
RELAX_TIME = 0.8
SPEED_UNIT = 0.05
FORCE_SCALE = 0.1
CONTACT_GAIN = 1.0
GRAVITY_STEP = 0.1


F32 = jnp.float32
BF16 = jnp.bfloat16
SIDES = [[[i for i, c in enumerate(LATTICE) if c[dim] == sign] for sign in (-1, 1)] for dim in range(3)]
Z_DIRS = SIDES[2][1] + SIDES[2][0]
FACES = [(1, 0, 0), (-1, 0, 0), (0, 1, 0), (0, -1, 0), (0, 0, 1), (0, 0, -1)]
NT = (((1,), (1,)), ((), ()))


def outgoing(dim, sign):
    return SIDES[dim][1 if sign > 0 else 0]


def find(vector):
    return LATTICE.index(tuple(vector))


def split3(value):
    high = value.astype(BF16).astype(F32)
    rest = value - high
    middle = rest.astype(BF16).astype(F32)
    return high, middle, rest - middle


def solid_share(fraction, slots, touches):
    return jnp.where(
        slots < touches,
        fraction * (RELAX_TIME - 0.5) / (1.0 - fraction + (RELAX_TIME - 0.5)),
        0.0,
    )


def moments(f):
    density = f[0]
    for i in range(1, 19):
        density = density + f[i]
    momentum = []
    for dim in range(3):
        total = None
        for i in outgoing(dim, 1):
            pair = f[i] - f[OPPOSITE[i]]
            total = pair if total is None else total + pair
        momentum.append(total)
    return density, momentum


def sums_kernel(
    source, fraction, slots, particles, touch, packets, vals, pop, arrivals,
    *, span_x, span_y, touches,
):
    width = pop.shape[2]
    fetches = []
    for x in range(span_x):
        part = pl.ds(x * span_y, span_y)
        fetches.append(
            pltpu.make_async_copy(source.at[:, part], pop.at[:, part], arrivals.at[x])
        )
        fetches[x].start()
    for x in range(span_x):
        rows = pl.ds(x * span_y, span_y)
        fetches[x].wait()
        f = [pop[i, rows, :] for i in range(19)]
        density, momentum = moments(f)
        share = solid_share(fraction[rows, :], slots[rows, :], touches)
        for q, field in enumerate(momentum + [density]):
            for s, part in enumerate(split3(share * field)):
                vals[pl.ds(x * span_y * 16 + s * 4 + q, span_y, stride=16), :] = part
        for j in range(12, 16):
            vals[pl.ds(x * span_y * 16 + j, span_y, stride=16), :] = jnp.zeros((span_y, width), F32)
    labels = lax.broadcasted_iota(jnp.int32, (touches, width), 0)
    group = 8

    def step(turn, total):
        block = slots[pl.ds(turn * group, group), :]
        left = []
        right = []
        for r in range(group):
            left.append(vals[pl.ds((turn * group + r) * 16, 16), :].astype(BF16))
            right.append(jnp.where(block[r : r + 1, :] == labels, 1.0, 0.0).astype(BF16))
        return total + lax.dot_general(
            jnp.concatenate(left, axis=1),
            jnp.concatenate(right, axis=1),
            NT,
            preferred_element_type=F32,
        )

    turns = span_x * span_y // group
    total = lax.fori_loop(0, turns, step, jnp.zeros((16, touches), F32), unroll=2)
    sums = total[0:4] + total[4:8] + total[8:12]
    halves = touches // width
    parts = [particles[...], touch[...].astype(F32)]
    for h in range(halves):
        parts.append(sums[:, h * width : (h + 1) * width])
    packet = jnp.concatenate(parts, axis=0)
    for n in range(packets.shape[0]):
        packets[n, :, :] = packet


def lookup(table, index):
    return jnp.take_along_axis(table, index, axis=1)


def step_kernel(
    place, pop, fraction, slots, packets, touch, contacts, code, slot,
    relaxed, send, z_up, z_down, stay, speeds, columns,
    *, span_x, span_y, touches, mesh_shape,
):
    width = pop.shape[2]
    halves = touches // width
    neighbours = contacts.shape[0]
    n_x, n_y, n_z = mesh_shape
    lane = lax.broadcasted_iota(jnp.int32, (8, width), 1)
    sub = lax.broadcasted_iota(jnp.int32, (8, width), 0)
    base = packets.shape[1]
    me = (place[0] * n_y + place[1]) * n_z + place[2]
    own = packets[me, 0:8, :]
    tables = []
    labels = lax.broadcasted_iota(jnp.int32, (width, width), 0)
    force = [jnp.zeros((24, width), F32) for h in range(halves)]
    touched = [jnp.zeros((8, width), F32) for h in range(halves)]
    touch_entries = [touch[h : h + 1, :] for h in range(halves)]
    touch_code = [jnp.broadcast_to(t // width, (8, width)) for t in touch_entries]
    touch_slot = [jnp.broadcast_to(t % width, (8, width)) for t in touch_entries]
    contact_all = contacts[...]
    contact_code = contact_all // width
    contact_slot = contact_all % width
    picked = [jnp.zeros((8, width), F32) for n in range(neighbours)]
    shifts = (span_x / R, span_y / R, width / R)
    for c in range(27):
        o = (c // 9 - 1, c // 3 % 3 - 1, c % 3 - 1)
        p = [place[k] + o[k] for k in range(3)]
        valid = (
            (p[0] >= 0) & (p[0] < n_x) & (p[1] >= 0) & (p[1] < n_y) & (p[2] >= 0) & (p[2] < n_z)
        )
        index = jnp.where(valid, (p[0] * n_y + p[1]) * n_z + p[2], me)
        keep = valid.astype(F32)
        record = packets[index, 0:8, :] * keep
        for h in range(halves):
            got = lookup(record, touch_slot[h])
            touched[h] = jnp.where(touch_code[h] == c, got, touched[h])
        offset = jnp.where(sub == 0, o[0] * shifts[0], jnp.where(sub == 1, o[1] * shifts[1], jnp.where(sub == 2, o[2] * shifts[2], 0.0)))
        shifted = record + offset
        for n in range(neighbours):
            got = lookup(shifted, jnp.broadcast_to(contact_slot[n : n + 1, :], (8, width)))
            picked[n] = jnp.where(jnp.broadcast_to(contact_code[n : n + 1, :], (8, width)) == c, got, picked[n])
        entries = packets[index, 6 : 6 + halves, :].astype(jnp.int32)
        mine = jnp.where(entries // width == 26 - c, entries % width, -1)
        for h in range(halves):
            part = packets[index, 6 + halves + 4 * h : 10 + halves + 4 * h, :] * keep
            part = jnp.concatenate([part, jnp.zeros((4, width), F32)], axis=0)
            left = jnp.concatenate(list(split3(part)), axis=0).astype(BF16)
            right = jnp.where(mine[h : h + 1, :] == labels, 1.0, 0.0).astype(BF16)
            force[h] = force[h] + lax.dot_general(left, right, NT, preferred_element_type=F32)
    total = force[0]
    for h in range(1, halves):
        total = total + force[h]
    total = total[0:8] + total[8:16] + total[16:24]

    contact_force = jnp.zeros((8, width), F32)
    for n in range(neighbours):
        separation = jnp.where(sub < 3, own - picked[n], 0.0)
        square = jnp.sum(separation * separation, axis=0, keepdims=True)
        soften = 1.0 + 0.25 * square
        valid = jnp.where(contact_all[n : n + 1, :] < 27 * width, CONTACT_GAIN, 0.0)
        contact_force = contact_force + separation * (valid / (soften * soften))
    position = own[0:3]
    velocity = own[3:6]
    hydro = total[0:3] - SPEED_UNIT * velocity * total[3:4]
    gravity = jnp.where(sub[0:3] == 2, GRAVITY_STEP, 0.0)
    velocity_new = velocity + FORCE_SCALE * hydro + contact_force[0:3] - gravity
    position_new = position + velocity_new * (SPEED_UNIT / R)
    record = jnp.concatenate([position_new, velocity_new, jnp.zeros((2, width), F32)], axis=0)
    placing = jnp.where(slot[...] == labels, 1.0, 0.0).astype(BF16)
    arrive = []
    for o in [(0, 0, 0)] + FACES:
        offset = jnp.where(sub == 0, o[0] * shifts[0], jnp.where(sub == 1, o[1] * shifts[1], jnp.where(sub == 2, o[2] * shifts[2], 0.0)))
        chosen = jnp.where(code[...] == 13 + 9 * o[0] + 3 * o[1] + o[2], record - offset, 0.0)
        left = jnp.concatenate(list(split3(chosen)), axis=0).astype(BF16)
        out = lax.dot_general(left, placing, NT, preferred_element_type=F32)
        arrive.append(out[0:8] + out[8:16] + out[16:24])
    stay[...] = arrive[0]

    for h in range(halves):
        speeds[h, :, :] = SPEED_UNIT * touched[h]
    lane_y = lax.broadcasted_iota(jnp.int32, (span_y, width), 1)

    def slab(x, carry):
        rows = pl.ds(pl.multiple_of(x * span_y, span_y), span_y)
        f = [pop[i, rows, :] for i in range(19)]
        density, momentum = moments(f)
        index = slots[rows, :]
        share = solid_share(fraction[rows, :], index, touches)
        solid = []
        for dim in range(3):
            value = jnp.zeros((span_y, width), F32)
            for h in range(halves):
                line = jnp.broadcast_to(speeds[h, 3 + dim : 4 + dim, :], (span_y, width))
                got = lookup(line, index % width)
                value = jnp.where(index // width == h, got, value)
            solid.append(value)
        u = [m / density for m in momentum]
        rate = (1.0 - share) / RELAX_TIME
        fluid_base = 1.0 - 1.5 * (u[0] * u[0] + u[1] * u[1] + u[2] * u[2])
        solid_base = 1.0 - 1.5 * (solid[0] * solid[0] + solid[1] * solid[1] + solid[2] * solid[2])

        def project(i, v):
            value = None
            for dim in range(3):
                if LATTICE[i][dim]:
                    term = v[dim] if LATTICE[i][dim] > 0 else -v[dim]
                    value = term if value is None else value + term
            return value

        packed = jnp.zeros((span_y, width), F32)
        for i in range(19):
            j = OPPOSITE[i]
            if j < i:
                continue
            scale = WEIGHTS[i] * density
            if i == 0:
                fluid = scale * fluid_base
                results = [(0, f[0] - rate * (f[0] - fluid) + share * (scale * solid_base - fluid))]
            else:
                pu = project(i, u)
                ps = project(i, solid)
                even_u = fluid_base + 4.5 * pu * pu
                even_s = solid_base + 4.5 * ps * ps
                eq_i = scale * (even_u + 3.0 * pu)
                eq_j = scale * (even_u - 3.0 * pu)
                solid_i = scale * (even_s + 3.0 * ps)
                solid_j = scale * (even_s - 3.0 * ps)
                swap = f[j] - f[i]
                results = [
                    (i, f[i] - rate * (f[i] - eq_i) + share * (swap + solid_i - eq_j)),
                    (j, f[j] - rate * (f[j] - eq_j) + share * (solid_j - swap - eq_i)),
                ]
            for d, value in results:
                relaxed[d, rows, :] = value
                if LATTICE[d][2]:
                    k = Z_DIRS.index(d)
                    at = width - 1 if LATTICE[d][2] > 0 else 0
                    packed = jnp.where(lane_y == k, pltpu.roll(value, (k - at) % width, 1), packed)
        columns[rows, :] = packed
        return carry

    lax.fori_loop(0, span_x, slab, 0)
    z_rows = columns[...].T[0:16, :]
    z_up[0:8, :] = arrive[5]
    z_up[8:16, :] = jnp.concatenate([z_rows[0:5], jnp.zeros((3, width), F32)], axis=0)
    z_down[0:8, :] = arrive[6]
    z_down[8:16, :] = jnp.concatenate([z_rows[5:10], jnp.zeros((3, width), F32)], axis=0)
    send[...] = jnp.zeros(send.shape, F32)
    for o_x in (-1, 0, 1):
        for o_y in (-1, 0, 1):
            if o_x == 0 and o_y == 0:
                continue
            p_x = place[0] + o_x
            p_y = place[1] + o_y
            valid = (p_x >= 0) & (p_x < n_x) & (p_y >= 0) & (p_y < n_y)

            @pl.when(valid)
            def fill(o_x=o_x, o_y=o_y, index=p_x * n_y + p_y):
                x_at = span_x - 1 if o_x > 0 else 0
                y_at = span_y - 1 if o_y > 0 else 0
                if o_x and o_y:
                    row = x_at * span_y + y_at
                    send[index, 8:9, :] = relaxed[find((o_x, o_y, 0)), row : row + 1, :]
                    return
                n = FACES.index((o_x, o_y, 0))
                up = Z_DIRS.index(find((o_x, o_y, 1)))
                down = Z_DIRS.index(find((o_x, o_y, -1)))
                send[index, 0:8, :] = jnp.concatenate(
                    [arrive[1 + n][0:6], z_rows[up : up + 1], z_rows[down : down + 1]], axis=0
                )
                if o_x:
                    for k, d in enumerate(outgoing(0, o_x)):
                        send[index, 8 + k * span_y : 8 + (k + 1) * span_y, :] = relaxed[
                            d, x_at * span_y : (x_at + 1) * span_y, :
                        ]
                else:
                    for k, d in enumerate(outgoing(1, o_y)):
                        send[index, 8 + k * span_x : 8 + (k + 1) * span_x, :] = relaxed[
                            d, pl.ds(y_at, span_x, stride=span_y), :
                        ]


def locators(place, mesh_shape):
    def neighbour(o_x, o_y):
        p_x = jnp.clip(place[0] + o_x, 0, mesh_shape[0] - 1)
        p_y = jnp.clip(place[1] + o_y, 0, mesh_shape[1] - 1)
        return p_x * mesh_shape[1] + p_y

    def inside(axis, sign):
        p = place[axis] + sign
        return (p >= 0) & (p < mesh_shape[axis])

    return neighbour, inside


def pass_on(place, relaxed, got, filler, out, staged, sent, dirs, span_x, span_y, mesh_shape):
    width = relaxed.shape[2]
    neighbour, inside = locators(place, mesh_shape)
    lane = lax.broadcasted_iota(jnp.int32, (span_y, width), 1)
    line = lax.broadcasted_iota(jnp.int32, (span_y, width), 0)
    copies = []
    for n, d in enumerate(dirs):
        c_x, c_y, c_z = LATTICE[d]
        y_in = inside(1, -c_y) if c_y else None
        z_in = inside(2, -c_z) if c_z else None
        for x in range(span_x):
            x_from = x - c_x
            crosses = x_from < 0 or x_from >= span_x
            if crosses:
                k = outgoing(0, c_x).index(d)
                value = got[neighbour(-c_x, 0), 8 + k * span_y : 8 + (k + 1) * span_y, :]
            else:
                value = relaxed[d, x_from * span_y : (x_from + 1) * span_y, :]
            outside = None
            if c_y:
                if crosses:
                    row = got[neighbour(-c_x, -c_y), 8:9, :]
                else:
                    at = 8 + outgoing(1, c_y).index(d) * span_x + x_from
                    row = got[neighbour(0, -c_y), at : at + 1, :]
                at_edge = line == (0 if c_y > 0 else span_y - 1)
                value = jnp.where(at_edge, row, pltpu.roll(value, c_y % span_y, 0))
                outside = at_edge & jnp.logical_not(y_in)
            if c_z:
                target = 0 if c_z > 0 else width - 1
                fill = pltpu.roll(
                    filler[x * span_y : (x + 1) * span_y, :], (target - Z_DIRS.index(d)) % width, 1
                )
                at_edge = lane == target
                value = jnp.where(at_edge, fill, pltpu.roll(value, c_z % width, 1))
                z_out = at_edge & jnp.logical_not(z_in)
                outside = z_out if outside is None else outside | z_out
            if crosses:
                x_out = jnp.broadcast_to(jnp.logical_not(inside(0, -c_x)), (span_y, width))
                outside = x_out if outside is None else outside | x_out
            if outside is not None:
                back = relaxed[OPPOSITE[d], x * span_y : (x + 1) * span_y, :]
                value = jnp.where(outside, back, value)
            staged[n, x * span_y : (x + 1) * span_y, :] = value
        copies.append(pltpu.make_async_copy(staged.at[n], out.at[d], sent.at[n]))
        copies[n].start()
    for copy in copies:
        copy.wait()


def flat_kernel(place, relaxed, got, out, staged, sent, *, span_x, span_y, mesh_shape):
    dirs = [d for d in range(19) if LATTICE[d][2] == 0]
    pass_on(place, relaxed, got, None, out, staged, sent, dirs, span_x, span_y, mesh_shape)


def pass_kernel(
    place, relaxed, got, z_below, z_above, stay, unused, out, particles, filler, staged, sent,
    *, span_x, span_y, mesh_shape,
):
    cells = span_x * span_y
    neighbour, inside = locators(place, mesh_shape)
    arrived = stay[...] + z_below[0:8, :] + z_above[0:8, :]
    for o_x, o_y, o_z in FACES[:4]:
        axis = 0 if o_x else 1
        keep = inside(axis, o_x + o_y)
        arrived = arrived + jnp.where(keep, got[neighbour(o_x, o_y), 0:8, :], 0.0)
    particles[...] = arrived[0:6]

    lane1 = lax.broadcasted_iota(jnp.int32, (1, cells), 1)
    fills = []
    for d in Z_DIRS:
        c_x, c_y, c_z = LATTICE[d]
        source = z_below if c_z > 0 else z_above
        k = outgoing(2, c_z).index(d)
        row = source[8 + k : 9 + k, :]
        if c_x or c_y:
            edge = source[pl.ds(16 + neighbour(-c_x, -c_y), 1), :]
            if c_x:
                row = pltpu.roll(row, (c_x * span_y) % cells, 1)
                edge = pltpu.roll(edge, (c_x * span_y) % cells, 1)
                at_edge = lane1 < span_y if c_x > 0 else lane1 >= cells - span_y
            else:
                row = pltpu.roll(row, c_y % cells, 1)
                edge = pltpu.roll(edge, (-c_y * (span_y - 1)) % cells, 1)
                at_edge = lane1 % span_y == (0 if c_y > 0 else span_y - 1)
            row = jnp.where(at_edge, edge, row)
        fills.append(row)
    stacked = jnp.concatenate(fills + [jnp.zeros((cells - len(fills), cells), F32)], axis=0)
    filler[...] = stacked.T
    pass_on(
        place, relaxed, got, filler, out, staged, sent, Z_DIRS, span_x, span_y, mesh_shape
    )


def shape_of(*dims):
    return jax.ShapeDtypeStruct(dims, F32)


VMEM = pl.BlockSpec(memory_space=pltpu.VMEM)
SMEM = pl.BlockSpec(memory_space=pltpu.SMEM)
HBM = pl.BlockSpec(memory_space=pltpu.HBM)


def call(kernel, outs, out_specs, scratch, specs, *operands, aliases={}):
    return pl.pallas_call(
        kernel,
        out_shape=outs,
        in_specs=specs,
        out_specs=out_specs,
        scratch_shapes=scratch,
        input_output_aliases=aliases,
    )(*operands)


def bind(kernel, **settings):
    def bound(*refs):
        return kernel(*refs, **settings)

    return bound


def body(
    populations, solid_fraction, intersection, touch, particles, contacts, dest_code, dest_slot
):
    unused, span_x, span_y, span_z = populations.shape
    particle_slots = particles.shape[4]
    touches = touch.shape[3]
    halves = touches // span_z
    neighbours = contacts.shape[3]
    cells = span_x * span_y
    axes = ("gx", "gy", "gz")
    mesh_shape = tuple(lax.axis_size(axis) for axis in axes)
    n_x, n_y, n_z = mesh_shape
    place = jnp.stack([lax.axis_index(axis) for axis in axes]).astype(jnp.int32)
    pop = populations.reshape(19, cells, span_z)
    fraction = solid_fraction.reshape(cells, span_z)
    slots = intersection.reshape(cells, span_z)
    records = particles.reshape(6, particle_slots)
    touch_rows = touch.reshape(halves, span_z)
    rows = 6 + 5 * halves
    copies = call(
        bind(sums_kernel, span_x=span_x, span_y=span_y, touches=touches),
        shape_of(n_x * n_y * n_z, rows, span_z),
        VMEM,
        [
            pltpu.VMEM((cells * 16, span_z), F32),
            pltpu.VMEM((19, cells, span_z), F32),
            pltpu.SemaphoreType.DMA((span_x,)),
        ],
        [HBM] + [VMEM] * 4,
        pop, fraction, slots, records, touch_rows,
    )
    packets = lax.all_to_all(copies, axes, 0, 0)
    chunk = 8 + 5 * max(span_x, span_y)
    relaxed, send, z_up, z_down, stay = call(
        bind(step_kernel, span_x=span_x, span_y=span_y, touches=touches, mesh_shape=mesh_shape),
        (
            shape_of(19, cells, span_z),
            shape_of(n_x * n_y, chunk, span_z),
            shape_of(16, span_z),
            shape_of(16, span_z),
            shape_of(8, span_z),
        ),
        (VMEM,) * 5,
        [pltpu.VMEM((halves, 8, span_z), F32), pltpu.VMEM((cells, span_z), F32)],
        [SMEM] + [VMEM] * 8,
        place, pop, fraction, slots, packets, touch_rows,
        contacts.reshape(neighbours, particle_slots),
        dest_code.reshape(1, particle_slots), dest_slot.reshape(1, particle_slots),
    )
    got = lax.all_to_all(send, ("gx", "gy"), 0, 0)
    up = [(i, i + 1) for i in range(n_z - 1)]
    down = [(j, i) for i, j in up]
    z_below = lax.ppermute(jnp.concatenate([z_up, got[:, 6]]), "gz", up)
    z_above = lax.ppermute(jnp.concatenate([z_down, got[:, 7]]), "gz", down)
    flat = call(
        bind(flat_kernel, span_x=span_x, span_y=span_y, mesh_shape=mesh_shape),
        shape_of(19, cells, span_z),
        HBM,
        [pltpu.VMEM((9, cells, span_z), F32), pltpu.SemaphoreType.DMA((9,))],
        [SMEM, VMEM, VMEM],
        place, relaxed, got,
    )
    passed, arrived = call(
        bind(pass_kernel, span_x=span_x, span_y=span_y, mesh_shape=mesh_shape),
        (shape_of(19, cells, span_z), shape_of(6, span_z)),
        (HBM, VMEM),
        [
            pltpu.VMEM((cells, cells), F32),
            pltpu.VMEM((10, cells, span_z), F32),
            pltpu.SemaphoreType.DMA((10,)),
        ],
        [SMEM] + [VMEM] * 5 + [HBM],
        place, relaxed, got, z_below, z_above, stay, flat,
        aliases={6: 0},
    )
    return passed.reshape(populations.shape), arrived.reshape(1, 1, 1, 6, particle_slots)


def solution(mesh):
    placed = (
        P(None, "gx", "gy", "gz"),
        P("gx", "gy", "gz"),
        P("gx", "gy", "gz"),
        P("gx", "gy", "gz", None),
        P("gx", "gy", "gz", None, None),
        P("gx", "gy", "gz", None, None),
        P("gx", "gy", "gz", None),
        P("gx", "gy", "gz", None),
    )
    return jax.shard_map(
        body,
        mesh=mesh,
        in_specs=placed,
        out_specs=(P(None, "gx", "gy", "gz"), P("gx", "gy", "gz", None, None)),
        check_vma=False,
    )
```

```python
import jax
import jax.numpy as jnp
from jax import lax
from jax.experimental import pallas as pl
from jax.experimental.pallas import tpu as pltpu
from jax.sharding import PartitionSpec as P

R = 8


LATTICE = [
    (0, 0, 0),
    (1, 0, 0),
    (-1, 0, 0),
    (0, 1, 0),
    (0, -1, 0),
    (0, 0, 1),
    (0, 0, -1),
    (1, 1, 0),
    (-1, -1, 0),
    (1, -1, 0),
    (-1, 1, 0),
    (1, 0, 1),
    (-1, 0, -1),
    (1, 0, -1),
    (-1, 0, 1),
    (0, 1, 1),
    (0, -1, -1),
    (0, 1, -1),
    (0, -1, 1),
]
OPPOSITE = [0, 2, 1, 4, 3, 6, 5, 8, 7, 10, 9, 12, 11, 14, 13, 16, 15, 18, 17]
WEIGHTS = [1.0 / 3.0] + [1.0 / 18.0] * 6 + [1.0 / 36.0] * 12
RELAX_TIME = 0.8
SPEED_UNIT = 0.05
FORCE_SCALE = 0.1
CONTACT_GAIN = 1.0
GRAVITY_STEP = 0.1


F32 = jnp.float32
BF16 = jnp.bfloat16
SIDES = [[[i for i, c in enumerate(LATTICE) if c[dim] == sign] for sign in (-1, 1)] for dim in range(3)]
Z_DIRS = SIDES[2][1] + SIDES[2][0]
FACES = [(1, 0, 0), (-1, 0, 0), (0, 1, 0), (0, -1, 0), (0, 0, 1), (0, 0, -1)]
NT = (((1,), (1,)), ((), ()))


def outgoing(dim, sign):
    return SIDES[dim][1 if sign > 0 else 0]


def find(vector):
    return LATTICE.index(tuple(vector))


def split3(value):
    high = value.astype(BF16).astype(F32)
    rest = value - high
    middle = rest.astype(BF16).astype(F32)
    return high, middle, rest - middle


def solid_share(fraction, slots, touches):
    return jnp.where(
        slots < touches,
        fraction * (RELAX_TIME - 0.5) / (1.0 - fraction + (RELAX_TIME - 0.5)),
        0.0,
    )


def moments(f):
    density = f[0]
    for i in range(1, 19):
        density = density + f[i]
    momentum = []
    for dim in range(3):
        total = None
        for i in outgoing(dim, 1):
            pair = f[i] - f[OPPOSITE[i]]
            total = pair if total is None else total + pair
        momentum.append(total)
    return density, momentum


def sums_kernel(
    source, fraction, slots, particles, touch, packets, vals, pop, arrivals,
    *, span_x, span_y, touches,
):
    width = pop.shape[2]
    fetches = []
    for x in range(span_x):
        part = pl.ds(x * span_y, span_y)
        fetches.append(
            pltpu.make_async_copy(source.at[:, part], pop.at[:, part], arrivals.at[x])
        )
        fetches[x].start()
    for x in range(span_x):
        rows = pl.ds(x * span_y, span_y)
        fetches[x].wait()
        f = [pop[i, rows, :] for i in range(19)]
        density, momentum = moments(f)
        share = solid_share(fraction[rows, :], slots[rows, :], touches)
        for q, field in enumerate(momentum + [density]):
            for s, part in enumerate(split3(share * field)):
                vals[pl.ds(x * span_y * 16 + s * 4 + q, span_y, stride=16), :] = part
        for j in range(12, 16):
            vals[pl.ds(x * span_y * 16 + j, span_y, stride=16), :] = jnp.zeros((span_y, width), F32)
    labels = lax.broadcasted_iota(jnp.int32, (touches, width), 0)
    group = 8

    def step(turn, total):
        block = slots[pl.ds(turn * group, group), :]
        left = []
        right = []
        for r in range(group):
            left.append(vals[pl.ds((turn * group + r) * 16, 16), :].astype(BF16))
            right.append(jnp.where(block[r : r + 1, :] == labels, 1.0, 0.0).astype(BF16))
        return total + lax.dot_general(
            jnp.concatenate(left, axis=1),
            jnp.concatenate(right, axis=1),
            NT,
            preferred_element_type=F32,
        )

    turns = span_x * span_y // group
    total = lax.fori_loop(0, turns, step, jnp.zeros((16, touches), F32), unroll=2)
    sums = total[0:4] + total[4:8] + total[8:12]
    halves = touches // width
    parts = [particles[i] for i in range(particles.shape[0])] + [touch[...].astype(F32)]
    for h in range(halves):
        parts.append(sums[:, h * width : (h + 1) * width])
    packet = jnp.concatenate(parts, axis=0)
    for n in range(packets.shape[0]):
        packets[n, :, :] = packet


def lookup(table, index):
    return jnp.take_along_axis(table, index, axis=1)


def step_kernel(
    place, pop, fraction, slots, packets, touch, contacts, code, slot,
    relaxed, send, z_up, z_down, stay, speeds, columns,
    *, span_x, span_y, touches, mesh_shape,
):
    width = pop.shape[2]
    halves = touches // width
    neighbours = contacts.shape[0]
    n_x, n_y, n_z = mesh_shape
    lane = lax.broadcasted_iota(jnp.int32, (8, width), 1)
    sub = lax.broadcasted_iota(jnp.int32, (8, width), 0)
    base = packets.shape[1]
    me = (place[0] * n_y + place[1]) * n_z + place[2]
    own = packets[me, 0:8, :]
    tables = []
    labels = lax.broadcasted_iota(jnp.int32, (width, width), 0)
    force = [jnp.zeros((24, width), F32) for h in range(halves)]
    touched = [jnp.zeros((8, width), F32) for h in range(halves)]
    touch_entries = [touch[h : h + 1, :] for h in range(halves)]
    touch_code = [jnp.broadcast_to(t // width, (8, width)) for t in touch_entries]
    touch_slot = [jnp.broadcast_to(t % width, (8, width)) for t in touch_entries]
    contact_all = contacts[...]
    contact_code = contact_all // width
    contact_slot = contact_all % width
    picked = [jnp.zeros((8, width), F32) for n in range(neighbours)]
    shifts = (span_x / R, span_y / R, width / R)
    for c in range(27):
        o = (c // 9 - 1, c // 3 % 3 - 1, c % 3 - 1)
        p = [place[k] + o[k] for k in range(3)]
        valid = (
            (p[0] >= 0) & (p[0] < n_x) & (p[1] >= 0) & (p[1] < n_y) & (p[2] >= 0) & (p[2] < n_z)
        )
        index = jnp.where(valid, (p[0] * n_y + p[1]) * n_z + p[2], me)
        keep = valid.astype(F32)
        record = packets[index, 0:8, :] * keep
        for h in range(halves):
            got = lookup(record, touch_slot[h])
            touched[h] = jnp.where(touch_code[h] == c, got, touched[h])
        offset = jnp.where(sub == 0, o[0] * shifts[0], jnp.where(sub == 1, o[1] * shifts[1], jnp.where(sub == 2, o[2] * shifts[2], 0.0)))
        shifted = record + offset
        for n in range(neighbours):
            got = lookup(shifted, jnp.broadcast_to(contact_slot[n : n + 1, :], (8, width)))
            picked[n] = jnp.where(jnp.broadcast_to(contact_code[n : n + 1, :], (8, width)) == c, got, picked[n])
        entries = packets[index, 6 : 6 + halves, :].astype(jnp.int32)
        mine = jnp.where(entries // width == 26 - c, entries % width, -1)
        for h in range(halves):
            part = packets[index, 6 + halves + 4 * h : 10 + halves + 4 * h, :] * keep
            part = jnp.concatenate([part, jnp.zeros((4, width), F32)], axis=0)
            left = jnp.concatenate(list(split3(part)), axis=0).astype(BF16)
            right = jnp.where(mine[h : h + 1, :] == labels, 1.0, 0.0).astype(BF16)
            force[h] = force[h] + lax.dot_general(left, right, NT, preferred_element_type=F32)
    total = force[0]
    for h in range(1, halves):
        total = total + force[h]
    total = total[0:8] + total[8:16] + total[16:24]

    contact_force = jnp.zeros((8, width), F32)
    for n in range(neighbours):
        separation = jnp.where(sub < 3, own - picked[n], 0.0)
        square = jnp.sum(separation * separation, axis=0, keepdims=True)
        soften = 1.0 + 0.25 * square
        valid = jnp.where(contact_all[n : n + 1, :] < 27 * width, CONTACT_GAIN, 0.0)
        contact_force = contact_force + separation * (valid / (soften * soften))
    position = own[0:3]
    velocity = own[3:6]
    hydro = total[0:3] - SPEED_UNIT * velocity * total[3:4]
    gravity = jnp.where(sub[0:3] == 2, GRAVITY_STEP, 0.0)
    velocity_new = velocity + FORCE_SCALE * hydro + contact_force[0:3] - gravity
    position_new = position + velocity_new * (SPEED_UNIT / R)
    record = jnp.concatenate([position_new, velocity_new, jnp.zeros((2, width), F32)], axis=0)
    placing = jnp.where(slot[...] == labels, 1.0, 0.0).astype(BF16)
    arrive = []
    for o in [(0, 0, 0)] + FACES:
        offset = jnp.where(sub == 0, o[0] * shifts[0], jnp.where(sub == 1, o[1] * shifts[1], jnp.where(sub == 2, o[2] * shifts[2], 0.0)))
        chosen = jnp.where(code[...] == 13 + 9 * o[0] + 3 * o[1] + o[2], record - offset, 0.0)
        left = jnp.concatenate(list(split3(chosen)), axis=0).astype(BF16)
        out = lax.dot_general(left, placing, NT, preferred_element_type=F32)
        arrive.append(out[0:8] + out[8:16] + out[16:24])
    stay[...] = arrive[0]

    for h in range(halves):
        speeds[h, :, :] = SPEED_UNIT * touched[h]
    lane_y = lax.broadcasted_iota(jnp.int32, (span_y, width), 1)

    def slab(x, carry):
        rows = pl.ds(pl.multiple_of(x * span_y, span_y), span_y)
        f = [pop[i, rows, :] for i in range(19)]
        density, momentum = moments(f)
        index = slots[rows, :]
        share = solid_share(fraction[rows, :], index, touches)
        solid = []
        for dim in range(3):
            value = jnp.zeros((span_y, width), F32)
            for h in range(halves):
                line = jnp.broadcast_to(speeds[h, 3 + dim : 4 + dim, :], (span_y, width))
                got = lookup(line, index % width)
                value = jnp.where(index // width == h, got, value)
            solid.append(value)
        u = [m / density for m in momentum]
        rate = (1.0 - share) / RELAX_TIME
        fluid_base = 1.0 - 1.5 * (u[0] * u[0] + u[1] * u[1] + u[2] * u[2])
        solid_base = 1.0 - 1.5 * (solid[0] * solid[0] + solid[1] * solid[1] + solid[2] * solid[2])

        def project(i, v):
            value = None
            for dim in range(3):
                if LATTICE[i][dim]:
                    term = v[dim] if LATTICE[i][dim] > 0 else -v[dim]
                    value = term if value is None else value + term
            return value

        packed = jnp.zeros((span_y, width), F32)
        for i in range(19):
            j = OPPOSITE[i]
            if j < i:
                continue
            scale = WEIGHTS[i] * density
            if i == 0:
                fluid = scale * fluid_base
                results = [(0, f[0] - rate * (f[0] - fluid) + share * (scale * solid_base - fluid))]
            else:
                pu = project(i, u)
                ps = project(i, solid)
                even_u = fluid_base + 4.5 * pu * pu
                even_s = solid_base + 4.5 * ps * ps
                eq_i = scale * (even_u + 3.0 * pu)
                eq_j = scale * (even_u - 3.0 * pu)
                solid_i = scale * (even_s + 3.0 * ps)
                solid_j = scale * (even_s - 3.0 * ps)
                swap = f[j] - f[i]
                results = [
                    (i, f[i] - rate * (f[i] - eq_i) + share * (swap + solid_i - eq_j)),
                    (j, f[j] - rate * (f[j] - eq_j) + share * (solid_j - swap - eq_i)),
                ]
            for d, value in results:
                relaxed[d, rows, :] = value
                if LATTICE[d][2]:
                    k = Z_DIRS.index(d)
                    at = width - 1 if LATTICE[d][2] > 0 else 0
                    packed = jnp.where(lane_y == k, pltpu.roll(value, (k - at) % width, 1), packed)
        columns[rows, :] = packed
        return carry

    lax.fori_loop(0, span_x, slab, 0)
    z_rows = columns[...].T[0:16, :]
    z_up[0:8, :] = arrive[5]
    z_up[8:16, :] = jnp.concatenate([z_rows[0:5], jnp.zeros((3, width), F32)], axis=0)
    z_down[0:8, :] = arrive[6]
    z_down[8:16, :] = jnp.concatenate([z_rows[5:10], jnp.zeros((3, width), F32)], axis=0)
    send[...] = jnp.zeros(send.shape, F32)
    for o_x in (-1, 0, 1):
        for o_y in (-1, 0, 1):
            if o_x == 0 and o_y == 0:
                continue
            p_x = place[0] + o_x
            p_y = place[1] + o_y
            valid = (p_x >= 0) & (p_x < n_x) & (p_y >= 0) & (p_y < n_y)

            @pl.when(valid)
            def fill(o_x=o_x, o_y=o_y, index=p_x * n_y + p_y):
                x_at = span_x - 1 if o_x > 0 else 0
                y_at = span_y - 1 if o_y > 0 else 0
                if o_x and o_y:
                    row = x_at * span_y + y_at
                    send[index, 8:9, :] = relaxed[find((o_x, o_y, 0)), row : row + 1, :]
                    return
                n = FACES.index((o_x, o_y, 0))
                up = Z_DIRS.index(find((o_x, o_y, 1)))
                down = Z_DIRS.index(find((o_x, o_y, -1)))
                send[index, 0:8, :] = jnp.concatenate(
                    [arrive[1 + n][0:6], z_rows[up : up + 1], z_rows[down : down + 1]], axis=0
                )
                if o_x:
                    for k, d in enumerate(outgoing(0, o_x)):
                        send[index, 8 + k * span_y : 8 + (k + 1) * span_y, :] = relaxed[
                            d, x_at * span_y : (x_at + 1) * span_y, :
                        ]
                else:
                    for k, d in enumerate(outgoing(1, o_y)):
                        send[index, 8 + k * span_x : 8 + (k + 1) * span_x, :] = relaxed[
                            d, pl.ds(y_at, span_x, stride=span_y), :
                        ]


def locators(place, mesh_shape):
    def neighbour(o_x, o_y):
        p_x = jnp.clip(place[0] + o_x, 0, mesh_shape[0] - 1)
        p_y = jnp.clip(place[1] + o_y, 0, mesh_shape[1] - 1)
        return p_x * mesh_shape[1] + p_y

    def inside(axis, sign):
        p = place[axis] + sign
        return (p >= 0) & (p < mesh_shape[axis])

    return neighbour, inside


def pass_on(place, relaxed, got, filler, out, staged, sent, dirs, span_x, span_y, mesh_shape):
    width = relaxed.shape[2]
    neighbour, inside = locators(place, mesh_shape)
    lane = lax.broadcasted_iota(jnp.int32, (span_y, width), 1)
    line = lax.broadcasted_iota(jnp.int32, (span_y, width), 0)
    copies = []
    for n, d in enumerate(dirs):
        c_x, c_y, c_z = LATTICE[d]
        y_in = inside(1, -c_y) if c_y else None
        z_in = inside(2, -c_z) if c_z else None
        for x in range(span_x):
            x_from = x - c_x
            crosses = x_from < 0 or x_from >= span_x
            if crosses:
                k = outgoing(0, c_x).index(d)
                value = got[neighbour(-c_x, 0), 8 + k * span_y : 8 + (k + 1) * span_y, :]
            else:
                value = relaxed[d, x_from * span_y : (x_from + 1) * span_y, :]
            outside = None
            if c_y:
                if crosses:
                    row = got[neighbour(-c_x, -c_y), 8:9, :]
                else:
                    at = 8 + outgoing(1, c_y).index(d) * span_x + x_from
                    row = got[neighbour(0, -c_y), at : at + 1, :]
                at_edge = line == (0 if c_y > 0 else span_y - 1)
                value = jnp.where(at_edge, row, pltpu.roll(value, c_y % span_y, 0))
                outside = at_edge & jnp.logical_not(y_in)
            if c_z:
                target = 0 if c_z > 0 else width - 1
                fill = pltpu.roll(
                    filler[x * span_y : (x + 1) * span_y, :], (target - Z_DIRS.index(d)) % width, 1
                )
                at_edge = lane == target
                value = jnp.where(at_edge, fill, pltpu.roll(value, c_z % width, 1))
                z_out = at_edge & jnp.logical_not(z_in)
                outside = z_out if outside is None else outside | z_out
            if crosses:
                x_out = jnp.broadcast_to(jnp.logical_not(inside(0, -c_x)), (span_y, width))
                outside = x_out if outside is None else outside | x_out
            if outside is not None:
                back = relaxed[OPPOSITE[d], x * span_y : (x + 1) * span_y, :]
                value = jnp.where(outside, back, value)
            staged[n, x * span_y : (x + 1) * span_y, :] = value
        copies.append(pltpu.make_async_copy(staged.at[n], out.at[d], sent.at[n]))
        copies[n].start()
    for copy in copies:
        copy.wait()


def flat_kernel(place, relaxed, got, out, staged, sent, *, span_x, span_y, mesh_shape):
    dirs = [d for d in range(19) if LATTICE[d][2] == 0]
    pass_on(place, relaxed, got, None, out, staged, sent, dirs, span_x, span_y, mesh_shape)


def pass_kernel(
    place, relaxed, got, z_below, z_above, stay, unused, out, particles, filler, staged, sent,
    *, span_x, span_y, mesh_shape,
):
    cells = span_x * span_y
    neighbour, inside = locators(place, mesh_shape)
    arrived = stay[...] + z_below[0:8, :] + z_above[0:8, :]
    for o_x, o_y, o_z in FACES[:4]:
        axis = 0 if o_x else 1
        keep = inside(axis, o_x + o_y)
        arrived = arrived + jnp.where(keep, got[neighbour(o_x, o_y), 0:8, :], 0.0)
    for i in range(particles.shape[0]):
        particles[i] = arrived[i : i + 1]

    lane1 = lax.broadcasted_iota(jnp.int32, (1, cells), 1)
    fills = []
    for d in Z_DIRS:
        c_x, c_y, c_z = LATTICE[d]
        source = z_below if c_z > 0 else z_above
        k = outgoing(2, c_z).index(d)
        row = source[8 + k : 9 + k, :]
        if c_x or c_y:
            edge = source[pl.ds(16 + neighbour(-c_x, -c_y), 1), :]
            if c_x:
                row = pltpu.roll(row, (c_x * span_y) % cells, 1)
                edge = pltpu.roll(edge, (c_x * span_y) % cells, 1)
                at_edge = lane1 < span_y if c_x > 0 else lane1 >= cells - span_y
            else:
                row = pltpu.roll(row, c_y % cells, 1)
                edge = pltpu.roll(edge, (-c_y * (span_y - 1)) % cells, 1)
                at_edge = lane1 % span_y == (0 if c_y > 0 else span_y - 1)
            row = jnp.where(at_edge, edge, row)
        fills.append(row)
    stacked = jnp.concatenate(fills + [jnp.zeros((cells - len(fills), cells), F32)], axis=0)
    filler[...] = stacked.T
    pass_on(
        place, relaxed, got, filler, out, staged, sent, Z_DIRS, span_x, span_y, mesh_shape
    )


def shape_of(*dims):
    return jax.ShapeDtypeStruct(dims, F32)


VMEM = pl.BlockSpec(memory_space=pltpu.VMEM)
SMEM = pl.BlockSpec(memory_space=pltpu.SMEM)
HBM = pl.BlockSpec(memory_space=pltpu.HBM)


def call(kernel, outs, out_specs, scratch, specs, *operands, aliases={}):
    return pl.pallas_call(
        kernel,
        out_shape=outs,
        in_specs=specs,
        out_specs=out_specs,
        scratch_shapes=scratch,
        input_output_aliases=aliases,
    )(*operands)


def bind(kernel, **settings):
    def bound(*refs):
        return kernel(*refs, **settings)

    return bound


def body(
    populations, solid_fraction, intersection, touch, particles, contacts, dest_code, dest_slot
):
    unused, span_x, span_y, span_z = populations.shape
    particle_slots = particles.shape[4]
    touches = touch.shape[3]
    halves = touches // span_z
    neighbours = contacts.shape[3]
    cells = span_x * span_y
    axes = ("gx", "gy", "gz")
    mesh_shape = tuple(lax.axis_size(axis) for axis in axes)
    n_x, n_y, n_z = mesh_shape
    place = jnp.stack([lax.axis_index(axis) for axis in axes]).astype(jnp.int32)
    pop = populations.reshape(19, cells, span_z)
    fraction = solid_fraction.reshape(cells, span_z)
    slots = intersection.reshape(cells, span_z)
    records = particles.reshape(6, 1, particle_slots)
    touch_rows = touch.reshape(halves, span_z)
    rows = 6 + 5 * halves
    copies = call(
        bind(sums_kernel, span_x=span_x, span_y=span_y, touches=touches),
        shape_of(n_x * n_y * n_z, rows, span_z),
        VMEM,
        [
            pltpu.VMEM((cells * 16, span_z), F32),
            pltpu.VMEM((19, cells, span_z), F32),
            pltpu.SemaphoreType.DMA((span_x,)),
        ],
        [HBM] + [VMEM] * 4,
        pop, fraction, slots, records, touch_rows,
    )
    packets = lax.all_to_all(copies, axes, 0, 0)
    chunk = 8 + 5 * max(span_x, span_y)
    relaxed, send, z_up, z_down, stay = call(
        bind(step_kernel, span_x=span_x, span_y=span_y, touches=touches, mesh_shape=mesh_shape),
        (
            shape_of(19, cells, span_z),
            shape_of(n_x * n_y, chunk, span_z),
            shape_of(16, span_z),
            shape_of(16, span_z),
            shape_of(8, span_z),
        ),
        (VMEM,) * 5,
        [pltpu.VMEM((halves, 8, span_z), F32), pltpu.VMEM((cells, span_z), F32)],
        [SMEM] + [VMEM] * 8,
        place, pop, fraction, slots, packets, touch_rows,
        contacts.reshape(neighbours, particle_slots),
        dest_code.reshape(1, particle_slots), dest_slot.reshape(1, particle_slots),
    )
    got = lax.all_to_all(send, ("gx", "gy"), 0, 0)
    up = [(i, i + 1) for i in range(n_z - 1)]
    down = [(j, i) for i, j in up]
    z_below = lax.ppermute(jnp.concatenate([z_up, got[:, 6]]), "gz", up)
    z_above = lax.ppermute(jnp.concatenate([z_down, got[:, 7]]), "gz", down)
    flat = call(
        bind(flat_kernel, span_x=span_x, span_y=span_y, mesh_shape=mesh_shape),
        shape_of(19, cells, span_z),
        HBM,
        [pltpu.VMEM((9, cells, span_z), F32), pltpu.SemaphoreType.DMA((9,))],
        [SMEM, VMEM, VMEM],
        place, relaxed, got,
    )
    passed, arrived = call(
        bind(pass_kernel, span_x=span_x, span_y=span_y, mesh_shape=mesh_shape),
        (shape_of(19, cells, span_z), shape_of(6, 1, span_z)),
        (HBM, VMEM),
        [
            pltpu.VMEM((cells, cells), F32),
            pltpu.VMEM((10, cells, span_z), F32),
            pltpu.SemaphoreType.DMA((10,)),
        ],
        [SMEM] + [VMEM] * 5 + [HBM],
        place, relaxed, got, z_below, z_above, stay, flat,
        aliases={6: 0},
    )
    return passed.reshape(populations.shape), arrived.reshape(1, 1, 1, 6, particle_slots)


def solution(mesh):
    placed = (
        P(None, "gx", "gy", "gz"),
        P("gx", "gy", "gz"),
        P("gx", "gy", "gz"),
        P("gx", "gy", "gz", None),
        P("gx", "gy", "gz", None, None),
        P("gx", "gy", "gz", None, None),
        P("gx", "gy", "gz", None),
        P("gx", "gy", "gz", None),
    )
    return jax.shard_map(
        body,
        mesh=mesh,
        in_specs=placed,
        out_specs=(P(None, "gx", "gy", "gz"), P("gx", "gy", "gz", None, None)),
        check_vma=False,
    )
```
